512 devices in a mesh: group: 8 (over z), leaf: 64 (over x, y, core).
Axes of the slice: x: 4, y: 8, z: 8, core: 2. Of those that a mesh axis runs over, the one named last changes fastest.
Arguments:
- points: bfloat16 [524288, 64], P(('group', 'leaf')), may hold values from -6 to 6
- weights: bfloat16 [524288, 128], P(('group', 'leaf')), may hold values from -6 to 6
- interp: bfloat16 [524288, 256], P(('group', 'leaf')), may hold values from -0.1875 to 0.1875
- cluster_interp: bfloat16 [131072, 512], P(('group', 'leaf')), may hold values from -0.09375 to 0.09375
- skeleton_rows: int32 [512, 256], P(('group', 'leaf')), may hold values from 0 to 1023, as said below
- near_flags: int32 [512, 5], P(('group', 'leaf')), may hold values from 0 to 1, as said below
- cluster_rows: int32 [32, 512], P('group'), may hold values from 0 to 4095, as said below
Outputs:
- potential: bfloat16 [524288, 128], P(('group', 'leaf'))
The draws below stay inside these ranges and needn't reach their ends.
Inputs may be any that keep to these rules, and one draw needn't show every extreme that they name: `skeleton_rows`: within a row the values are distinct. `near_flags`: the middle column is 1; a column is 0 where the leaf it names lies outside the leaf's group. `cluster_rows`: within a row the values are distinct.
All inputs are finite; a program needn't handle non-finite values.
Results may differ from the reference program's by a relative error of at most 0.0063.
Values may be sent and summed in bfloat16 or wider, within the bound.
A program may use at most 64 MiB of HBM per device.

```python
import jax
import jax.numpy as jnp
from jax import lax

F = 64
R = 128
LEAF = 1024
SK = 256
CSK = 512
REACH = 2
LEAVES = 512
CLUSTERS = 32
NPTS = 524288
N_GROUP = 8
N_LEAF = 64


def draw_skeleton_rows(key, part):
    keys = jax.random.split(jax.random.fold_in(key, 3), LEAVES)
    return jax.vmap(lambda single: jax.random.permutation(single, LEAF)[:SK])(keys).astype(jnp.int32)


def draw_cluster_rows(key, part):
    keys = jax.random.split(jax.random.fold_in(key, 5), CLUSTERS)
    return jax.vmap(lambda single: jax.random.permutation(single, 16 * SK)[:CSK])(keys).astype(jnp.int32)


def draw_near_flags(key, part):
    first_key, second_key = jax.random.split(jax.random.fold_in(key, 11))
    flag_count = 2 * REACH + 1
    levels = jax.random.randint(first_key, (LEAVES, 1), 0, 5)
    rolled = jax.random.randint(second_key, (LEAVES, flag_count), 0, 4)
    offsets = jnp.arange(flag_count, dtype=jnp.int32)[None, :] - REACH
    places = jnp.arange(LEAVES, dtype=jnp.int32)[:, None] % N_LEAF
    inside = (places + offsets >= 0) & (places + offsets < N_LEAF)
    chosen = jnp.where(inside & (rolled < levels), 1, 0)
    return jnp.where(offsets == 0, 1, chosen).astype(jnp.int32)


def steps_of(rng, extent, pieces, low, largest):
    level, own = 1.0, jax.random.fold_in(rng, 6)
    for dim, blocks in pieces:
        heights = jnp.exp(jax.random.uniform(jax.random.fold_in(own, dim), (blocks,), jnp.float32, low / len(pieces), largest / len(pieces)))
        level = level * jnp.repeat(heights, extent[dim] // blocks).reshape([-1 if axis == dim else 1 for axis in range(len(extent))])
    return level


def normal_values(stream_key, shape, spread, bound, pieces=(), kind=jnp.bfloat16):
    values = jax.random.normal(stream_key, shape, jnp.float32) * spread
    if len(pieces) > 0:
        values = steps_of(stream_key, shape, pieces, -0.22, 0.18) * values
    return jnp.clip(values, min=-bound, max=bound).astype(kind)


def setup_inputs(seed: int = 0) -> dict:
    seeds = jax.random.split(jax.random.key(seed), 8)
    points = normal_values(seeds[0], (NPTS, F), 1.0, 6.0, ((0, 512),))
    weights = normal_values(seeds[1], (NPTS, R), 1.0, 6.0, ((0, 512),))
    interp = normal_values(seeds[2], (NPTS, SK), LEAF ** -0.5, 0.1875, ((0, 512),))
    cluster_interp = normal_values(seeds[3], (LEAVES * SK, CSK), (16 * SK) ** -0.5, 0.09375, ((0, 512),))
    skeleton_rows = draw_skeleton_rows(jax.random.fold_in(seeds[7], 71), 0)
    near_flags = draw_near_flags(jax.random.fold_in(seeds[7], 71), 0)
    cluster_rows = draw_cluster_rows(jax.random.fold_in(seeds[7], 71), 0)
    return dict(points=points, weights=weights, interp=interp, cluster_interp=cluster_interp, skeleton_rows=skeleton_rows, near_flags=near_flags, cluster_rows=cluster_rows)


def kernel_tile(targets, sources):
    target_sq_norm_values = jnp.sum(jnp.square(targets.astype(jnp.float32)), axis=1)
    source_norm = jnp.sum(jnp.square(sources.astype(jnp.float32)), axis=1)
    inner_term = lax.dot_general(targets, sources, (((1,), (1,)), ((), ())), preferred_element_type=jnp.float32)
    scaled = (target_sq_norm_values[:, None] + source_norm[None, :] - 2.0 * inner_term) * (2.0 / targets.shape[1])
    return jnp.exp(-scaled).astype(jnp.bfloat16)


def reference(points, weights, interp, cluster_interp, skeleton_rows, near_flags, cluster_rows):
    leaf_nodes = N_GROUP * N_LEAF
    clusters = leaf_nodes // 16
    leaf_points = points.reshape(leaf_nodes, LEAF, F)
    leaf_weight_values = weights.reshape(leaf_nodes, LEAF, R)
    leaf_interpolant = interp.reshape(leaf_nodes, LEAF, SK)
    skeleton = jnp.take_along_axis(leaf_points, skeleton_rows.astype(jnp.int32)[:, :, None], axis=1)
    skeleton_charges = jnp.einsum("cbm,cbx->cmx", leaf_interpolant.astype(jnp.float32), leaf_weight_values.astype(jnp.float32)).astype(jnp.bfloat16)
    cluster_mass = jnp.einsum("cajk,cajr->ckr", cluster_interp.reshape(clusters, 16, SK, CSK).astype(jnp.float32), skeleton_charges.reshape(clusters, 16, SK, R).astype(jnp.float32)).astype(jnp.bfloat16)
    cluster_points = jnp.take_along_axis(skeleton.reshape(clusters, 16 * SK, F), cluster_rows.astype(jnp.int32)[:, :, None], axis=1)
    flattened_points = cluster_points.reshape(clusters * CSK, F)
    flat_mass = cluster_mass.reshape(clusters * CSK, R)
    per_group = (N_LEAF // 16) * CSK
    row_group = jnp.arange(clusters * CSK, dtype=jnp.int32) // per_group
    flag_count = 2 * REACH + 1
    offsets = jnp.arange(flag_count, dtype=jnp.int32) - REACH

    def one_leaf(target):
        group_index = target // N_LEAF
        place = target % N_LEAF
        nearby_row = near_flags[target]
        near_field = jnp.zeros((LEAF, R), jnp.float32)
        for column in range(flag_count):
            source = jnp.clip(target + column - REACH, 0, leaf_nodes - 1).astype(jnp.int32)
            block_kernel = kernel_tile(leaf_points[target], leaf_points[source])
            near_field = near_field + nearby_row[column].astype(jnp.float32) * jnp.dot(block_kernel, leaf_weight_values[source], preferred_element_type=jnp.float32)
        sibling_points = lax.dynamic_slice_in_dim(skeleton, group_index * N_LEAF, N_LEAF, 0).reshape(N_LEAF * SK, F)
        sibling_mass = lax.dynamic_slice_in_dim(skeleton_charges, group_index * N_LEAF, N_LEAF, 0).reshape(N_LEAF * SK, R)
        distance = jnp.arange(N_LEAF * SK, dtype=jnp.int32) // SK - place
        listed = jnp.sum((distance[:, None] == offsets[None, :]).astype(jnp.int32) * nearby_row[None, :], axis=1)
        kept_rows = (1 - listed).astype(jnp.bfloat16)
        sibling = jnp.dot(kernel_tile(skeleton[target], sibling_points), sibling_mass * kept_rows[:, None], preferred_element_type=jnp.float32)
        far_rows = (row_group != group_index).astype(jnp.bfloat16)
        distant = jnp.dot(kernel_tile(skeleton[target], flattened_points), flat_mass * far_rows[:, None], preferred_element_type=jnp.float32)
        coarse_field = (sibling + distant).astype(jnp.bfloat16)
        return (near_field + jnp.dot(leaf_interpolant[target], coarse_field, preferred_element_type=jnp.float32)).astype(jnp.bfloat16)

    result = lax.map(one_leaf, jnp.arange(leaf_nodes, dtype=jnp.int32))
    return result.reshape(leaf_nodes * LEAF, R)
```

```python
import jax
import jax.numpy as jnp
from jax import lax
from jax.experimental import pallas as pl
from jax.experimental.pallas import tpu as pltpu
from jax.sharding import PartitionSpec as P

MESH = pl.DeviceIdType.MESH
F32, BF16 = jnp.float32, jnp.bfloat16

FEAT = 64
LANES = 128
LEAF = 1024
SK = 256
CSK = 512
NX, NY, NZ, NC = 4, 8, 8, 2
TAIL = 64
HOT = TAIL + 6
GATE = TAIL + 14
TROWS = 80
BIG = -30000.0
SIB = NX * NC * SK
PART = CSK // (NY * NC)
HALF = NX * (NZ - 1) * PART
DIST = NC * HALF


def row_ids(shape):
    return lax.broadcasted_iota(jnp.int32, shape, 0)


def lane_ids(shape):
    return lax.broadcasted_iota(jnp.int32, shape, 1)


def parts_of(norm):
    high = norm.astype(BF16).astype(F32)
    rest = norm - high
    mid = rest.astype(BF16).astype(F32)
    return high, mid, (rest - mid).astype(BF16).astype(F32)


def tile_product(targets, sources, mass):
    exponent = lax.dot_general(
        targets, sources, (((1,), (1,)), ((), ())), preferred_element_type=F32
    )
    return jnp.dot(jnp.exp(exponent).astype(BF16), mass, preferred_element_type=F32)


def kernel(
    pts_h, wts_h, itp_h, cin_h, skr_h, nfl_h, clr_h, out_ref,
    pts, itp, cin, skr, nfl, clr,
    near, near_tgt, near_acc,
    skel_t, tgt_out, tgt_in, tgt, src, acc,
    c_all, c1_out, c1_in, c2_out, c2_in, d_out,
    e_out, e_in,
    in_sem, c1_s, c1_r, c2_s, c2_r, a_s, a_r, bx_s, bx_r, bp_s, bp_r,
    d_s, d_r, dp_s, dp_r, f_s, f_r, e_s, e_r,
):
    z = lax.axis_index("group")
    leaf = lax.axis_index("leaf")
    x = lax.div(leaf, NY * NC)
    y = lax.rem(lax.div(leaf, NC), NY)
    c = lax.rem(leaf, NC)

    def place(xx, yy, cc):
        return xx * (NY * NC) + yy * NC + cc

    def at_y(k):
        return (z, place(x, lax.rem(y + k + NY, NY), c))

    def at_x(i):
        return (z, place(lax.rem(x + i, NX), y, c))

    def at_xz(i, k):
        return (lax.rem(z + k, NZ), place(lax.rem(x + i, NX), y, c))

    def beside(step):
        return (z, lax.rem(leaf + step + NX * NY * NC, NX * NY * NC))

    partner = (z, place(x, y, 1 - c))

    def remote(source, target, send, recv, device):
        return pltpu.make_async_remote_copy(
            src_ref=source, dst_ref=target, send_sem=send, recv_sem=recv,
            device_id=device, device_id_type=MESH,
        )

    ins = [
        pltpu.make_async_copy(pts_h, pts, in_sem.at[0]),
        pltpu.make_async_copy(skr_h, skr, in_sem.at[1]),
        pltpu.make_async_copy(nfl_h, nfl, in_sem.at[2]),
        pltpu.make_async_copy(wts_h, near.at[0, :, LANES:], in_sem.at[3]),
        pltpu.make_async_copy(itp_h, itp, in_sem.at[4]),
        pltpu.make_async_copy(cin_h, cin, in_sem.at[5]),
        pltpu.make_async_copy(clr_h, clr, in_sem.at[6]),
    ]
    for copy in ins:
        copy.start()

    barrier = pltpu.get_barrier_semaphore()
    friends = [at_y(k) for k in range(1, NY)] + [at_x(i) for i in range(1, NX)]
    friends += [at_xz(i, k) for i in range(NX) for k in range(1, NZ)]
    friends += [partner, beside(2), beside(-2)]
    for device in friends:
        pl.semaphore_signal(barrier, inc=1, device_id=device, device_id_type=MESH)

    ins[0].wait()
    ins[1].wait()
    ins[2].wait()
    coords = pts[...].astype(F32) * 0.25
    high, mid, low = parts_of(-0.5 * jnp.sum(coords * coords, axis=0, keepdims=True))
    rows = row_ids((16, LEAF))
    zero_rows = jnp.zeros((LANES - TROWS, LEAF), F32)
    ones = jnp.where((rows < 3) | (rows == 14), 1.0, 0.0)
    tail = jnp.where(rows == 3, high, jnp.where(rows == 4, mid, jnp.where(rows == 5, low, ones)))
    source_t = jnp.concatenate([coords, tail, zero_rows], axis=0)
    ones = jnp.where((rows >= 3) & (rows < 6), 1.0, 0.0)
    tail = jnp.where(rows == 0, high, jnp.where(rows == 1, mid, jnp.where(rows == 2, low, ones)))
    target_t = jnp.concatenate([coords, tail, zero_rows], axis=0)
    near[0, :, :LANES] = source_t.T.astype(BF16)
    near_tgt[...] = target_t.T.astype(BF16)

    picks = jnp.where(row_ids((LEAF, SK)) == skr[...], 1.0, 0.0).astype(BF16)
    skel_t[...] = jnp.dot(source_t.astype(BF16), picks, preferred_element_type=F32)

    flags = nfl[...].astype(F32)

    def flag_of(column):
        chosen = jnp.where(lane_ids(flags.shape) == column, flags, 0.0)
        return jnp.sum(chosen, axis=1, keepdims=True)

    rows = row_ids((16, SK))
    ones = jnp.where((rows >= 3) & (rows < 6), 1.0, 0.0)
    base = jnp.where(
        rows == 0, skel_t[67:68, :],
        jnp.where(rows == 1, skel_t[68:69, :], jnp.where(rows == 2, skel_t[69:70, :], ones)),
    )
    slot = rows - 6
    valid = (slot >= 0) & (slot < NX * NC)
    listed = [flag_of(column) for column in range(5)]
    for k in range(NY):
        there = lax.rem(y + k, NY)
        other = lax.shift_right_logical(slot, 1) * (NY * NC) + there * NC + (slot & 1)
        column = other - leaf + 2
        hidden = jnp.zeros((16, SK), F32)
        for j in range(5):
            hidden = jnp.where(valid & (column == j), listed[j], hidden)
        tgt_out[k, FEAT:TROWS, :] = (base + BIG * hidden).astype(BF16)
        tgt_out[k, 0:FEAT, :] = skel_t[0:FEAT, :].astype(BF16)

    hot = jnp.where(row_ids((LANES, SK)) == HOT + x * NC + c, 1.0, 0.0)
    src[0:SK, 0:LANES] = (skel_t[...] + hot).T.astype(BF16)

    ins[3].wait()
    ins[4].wait()
    charges = lax.dot_general(
        itp[...], near[0, :, LANES:], (((0,), (0,)), ((), ())), preferred_element_type=F32
    ).astype(BF16)
    src[0:SK, LANES:] = charges

    ins[5].wait()
    ins[6].wait()
    mine = row_ids((SK, CSK)) + lax.rem(leaf, NY * NC) * SK
    picks = jnp.where(mine == clr[pl.ds(x, 1), :], 1.0, 0.0).astype(BF16)
    chosen = jnp.dot(skel_t[...].astype(BF16), picks, preferred_element_type=F32).T
    spread = lax.dot_general(
        cin[...], charges, (((0,), (0,)), ((), ())), preferred_element_type=F32
    )
    for b in range(NY * NC):
        c_all[b, :, 0:LANES] = chosen[b * PART:(b + 1) * PART]
        c_all[b, :, LANES:] = spread[b * PART:(b + 1) * PART]
    for yy in range(NY):
        c1_out[yy] = c_all[yy * NC + (1 - c)].astype(BF16)

    pl.semaphore_wait(barrier, len(friends))

    sent = []

    def go(copy):
        copy.start()
        sent.append(copy)
        return copy

    c1 = go(remote(c1_out, c1_in, c1_s, c1_r, partner))
    ax = [
        go(remote(tgt_out.at[k], tgt_in.at[k], a_s.at[k], a_r.at[k], at_y(k)))
        for k in range(1, NY)
    ]
    own = src.at[0:SK]
    bx = [
        go(remote(own, src.at[i * SK:(i + 1) * SK], bx_s.at[i], bx_r.at[i], at_x(i)))
        for i in range(1, NX)
    ]

    def pass_on(i):
        return go(remote(
            src.at[i * SK:(i + 1) * SK], src.at[(NX + i) * SK:(NX + i + 1) * SK],
            bp_s.at[i], bp_r.at[i], partner,
        ))

    bp = [pass_on(0)]
    fx = [
        go(remote(near.at[0], near.at[1], f_s.at[0], f_r.at[0], partner)),
    ]

    c1.wait_recv()
    for yy in range(NY):
        c2_out[yy] = (c_all[yy * NC + c] + c1_in[yy].astype(F32)).astype(BF16)
    c2 = [
        go(remote(
            c2_out.at[lax.rem(y + k, NY)], c2_in.at[k], c2_s.at[k], c2_r.at[k], at_y(k)
        ))
        for k in range(1, NY)
    ]
    fx += [
        go(remote(near.at[0], near.at[3], f_s.at[1], f_r.at[1], beside(2))),
        go(remote(near.at[0], near.at[2], f_s.at[2], f_r.at[2], beside(-2))),
    ]

    def near_tile(slot_at, flag):
        gate = jnp.where(lane_ids((1, LANES)) == GATE, BIG * (1.0 - flag), 0.0).astype(BF16)
        return tile_product(
            near_tgt[...] + gate, near[slot_at, :, 0:LANES], near[slot_at, :, LANES:]
        )

    near_acc[...] = near_tile(0, listed[2])

    part = c_all[y * NC + c] + c1_in[y].astype(F32)
    for k in range(1, NY):
        c2[k - 1].wait_recv()
        part = part + c2_in[k].astype(F32)
    d_out[...] = part.astype(BF16)

    def d_slot(half, i, k):
        start = SIB + half * HALF + (i * (NZ - 1) + k - 1) * PART
        return src.at[start:start + PART]

    dx = [
        go(remote(
            d_out, d_slot(0, i, k), d_s.at[i * (NZ - 1) + k - 1],
            d_r.at[i * (NZ - 1) + k - 1], at_xz(i, k),
        ))
        for i in range(NX) for k in range(1, NZ)
    ]

    for i in range(1, NX):
        bx[i - 1].wait_recv()
        bp.append(pass_on(i))
    tgt_in[0] = tgt_out[0]
    for k in range(1, NY):
        ax[k - 1].wait_recv()
    for copy in bp:
        copy.wait_recv()

    pad = jnp.zeros((LANES - TROWS, SK), F32)

    def sibling_step(p, carry):
        for h in range(2):
            k = p * 2 + h
            block = jnp.concatenate([tgt_in[k].astype(F32), pad], axis=0)
            tgt[pl.ds(pl.multiple_of(k * SK, SK), SK), :] = block.T.astype(BF16)
        at = pl.ds(pl.multiple_of(p * 2 * SK, 2 * SK), 2 * SK)
        acc[at, :] = tile_product(tgt[at, :], src[0:SIB, 0:LANES], src[0:SIB, LANES:])
        return carry

    lax.fori_loop(0, NY // 2, sibling_step, 0)

    for i in range(NX):
        for k in range(1, NZ):
            dx[i * (NZ - 1) + k - 1].wait_recv()
    first = SIB + HALF
    dp = go(remote(
        src.at[SIB:first], src.at[first:SIB + DIST], dp_s, dp_r, partner
    ))

    fx[2].wait_recv()
    fx[1].wait_recv()
    fp = go(remote(near.at[2 + c], near.at[4], f_s.at[3], f_r.at[3], partner))

    dp.wait_recv()

    def e_copy(k):
        return remote(e_out.at[k], e_in.at[k], e_s.at[k], e_r.at[k], at_y(-k))

    def distant_step(step, carry):
        p = NY // 2 - 1 - step
        at = pl.ds(pl.multiple_of(p * 2 * SK, 2 * SK), 2 * SK)
        total = acc[at, :] + tile_product(
            tgt[at, :], src[SIB:, 0:LANES], src[SIB:, LANES:]
        )
        acc[at, :] = total
        for h in range(2):
            k = p * 2 + h
            e_out[k] = total[h * SK:(h + 1) * SK].astype(BF16)

            @pl.when(k > 0)
            def _():
                e_copy(k).start()

        return carry

    lax.fori_loop(0, NY // 2, distant_step, 0)

    fx[0].wait_recv()
    fp.wait_recv()

    def near_step(s, carry):
        side = jnp.where(c == 0, 3, 1)
        column = jnp.where(
            s == 1, side, jnp.where(s == 2, 4, jnp.where(s == 3, 0, 4 - side))
        )
        near_acc[...] += near_tile(s, flag_of(column))
        return carry

    lax.fori_loop(1, 5, near_step, 0)

    phi = acc[0:SK, :]
    for k in range(1, NY):
        e_copy(k).wait_recv()
        phi = phi + e_in[k].astype(F32)
    out_ref[...] = (
        near_acc[...] + jnp.dot(itp[...], phi.astype(BF16), preferred_element_type=F32)
    ).astype(BF16)

    for k in range(1, NY):
        e_copy(k).wait_send()
    for copy in sent:
        copy.wait_send()


def on_device(points, weights, interp, cluster_interp, skeleton_rows, near_flags, cluster_rows):
    vmem, dma = pltpu.VMEM, pltpu.SemaphoreType.DMA
    return pl.pallas_call(
        kernel,
        out_shape=jax.ShapeDtypeStruct(weights.shape, BF16),
        in_specs=[pl.BlockSpec(memory_space=pl.ANY)] * 7,
        out_specs=pl.BlockSpec(memory_space=pltpu.VMEM),
        scratch_shapes=[
            vmem((FEAT, LEAF), BF16),
            vmem((LEAF, SK), BF16),
            vmem((SK, CSK), BF16),
            vmem((1, SK), jnp.int32),
            vmem((1, 5), jnp.int32),
            vmem((NX, CSK), jnp.int32),
            vmem((5, LEAF, 2 * LANES), BF16),
            vmem((LEAF, LANES), BF16),
            vmem((LEAF, LANES), F32),
            vmem((LANES, SK), F32),
            vmem((NY, TROWS, SK), BF16),
            vmem((NY, TROWS, SK), BF16),
            vmem((NY * SK, LANES), BF16),
            vmem((SIB + DIST, 2 * LANES), BF16),
            vmem((NY * SK, LANES), F32),
            vmem((NY * NC, PART, 2 * LANES), F32),
            vmem((NY, PART, 2 * LANES), BF16),
            vmem((NY, PART, 2 * LANES), BF16),
            vmem((NY, PART, 2 * LANES), BF16),
            vmem((NY, PART, 2 * LANES), BF16),
            vmem((PART, 2 * LANES), BF16),
            vmem((NY, SK, LANES), BF16),
            vmem((NY, SK, LANES), BF16),
            dma((7,)),
            dma, dma,
            dma((NY,)), dma((NY,)),
            dma((NY,)), dma((NY,)),
            dma((NX,)), dma((NX,)),
            dma((NX,)), dma((NX,)),
            dma((NX * (NZ - 1),)), dma((NX * (NZ - 1),)),
            dma, dma,
            dma((4,)), dma((4,)),
            dma((NY,)), dma((NY,)),
        ],
        compiler_params=pltpu.CompilerParams(
            collective_id=0, has_side_effects=True, vmem_limit_bytes=60 << 20
        ),
        name="hier",
    )(points.T, weights, interp, cluster_interp, skeleton_rows, near_flags, cluster_rows)


def solution(mesh):
    placed = P(("group", "leaf"), None)
    return jax.shard_map(
        on_device,
        mesh=mesh,
        in_specs=(placed,) * 6 + (P("group", None),),
        out_specs=placed,
        check_vma=False,
    )
```

```python
import jax
import jax.numpy as jnp
from jax import lax
from jax.experimental import pallas as pl
from jax.experimental.pallas import tpu as pltpu
from jax.sharding import PartitionSpec as P

MESH = pl.DeviceIdType.MESH
F32, BF16 = jnp.float32, jnp.bfloat16

FEAT = 64
LANES = 128
LEAF = 1024
SK = 256
CSK = 512
NX, NY, NZ, NC = 4, 8, 8, 2
TAIL = 64
HOT = TAIL + 6
GATE = TAIL + 14
TROWS = 80
BIG = -30000.0
SIB = NX * NC * SK
PART = CSK // (NY * NC)
HALF = NX * (NZ - 1) * PART
DIST = NC * HALF


def row_ids(shape):
    return lax.broadcasted_iota(jnp.int32, shape, 0)


def lane_ids(shape):
    return lax.broadcasted_iota(jnp.int32, shape, 1)


def parts_of(norm):
    high = norm.astype(BF16).astype(F32)
    rest = norm - high
    mid = rest.astype(BF16).astype(F32)
    return high, mid, (rest - mid).astype(BF16).astype(F32)


def tile_product(targets, sources, mass):
    exponent = lax.dot_general(
        targets, sources, (((1,), (1,)), ((), ())), preferred_element_type=F32
    )
    return jnp.dot(jnp.exp(exponent).astype(BF16), mass, preferred_element_type=F32)


def kernel(
    pts_h, wts_h, itp_h, cin_h, skr_h, nfl_h, clr_h, out_ref,
    pts, itp, cin, skr, nfl, clr,
    near_pts, near_mass, near_tgt, near_acc,
    skel_t, tgt_in, tgt, sib_pts, sib_mass, far, acc,
    c_all, c1_out, c1_in, c2_out, c2_in, d_out,
    e_out, e_in, wrap,
    in_sem, c1_s, c1_r, c2_s, c2_r, a_s, a_r, bx_s, bx_r, bp_s, bp_r,
    dz_s, dz_r, dx_s, dx_r, dp_s, dp_r, f_s, f_r, e_s, e_r, w_s, w_r,
):
    z = lax.axis_index("group")
    leaf = lax.axis_index("leaf")
    x = lax.div(leaf, NY * NC)
    y = lax.rem(lax.div(leaf, NC), NY)
    c = lax.rem(leaf, NC)

    def place(xx, yy, cc):
        return xx * (NY * NC) + yy * NC + cc

    def at_y(k):
        return (z, place(x, lax.rem(y + k + NY, NY), c))

    def at_x(i):
        return (z, place(lax.rem(x + i, NX), y, c))

    def at_z(k):
        return (lax.rem(z + k, NZ), leaf)

    def beside(step):
        return (z, lax.rem(leaf + step + NX * NY * NC, NX * NY * NC))

    partner = (z, place(x, y, 1 - c))

    def remote(source, target, send, recv, device):
        return pltpu.make_async_remote_copy(
            src_ref=source, dst_ref=target, send_sem=send, recv_sem=recv,
            device_id=device, device_id_type=MESH,
        )

    ins = [
        pltpu.make_async_copy(pts_h, pts, in_sem.at[0]),
        pltpu.make_async_copy(skr_h, skr, in_sem.at[1]),
        pltpu.make_async_copy(wts_h, near_mass.at[0], in_sem.at[2]),
        pltpu.make_async_copy(itp_h, itp, in_sem.at[3]),
        pltpu.make_async_copy(cin_h, cin, in_sem.at[4]),
        pltpu.make_async_copy(clr_h, clr, in_sem.at[5]),
        pltpu.make_async_copy(nfl_h, nfl, in_sem.at[6]),
    ]
    for copy in ins:
        copy.start()

    barrier = pltpu.get_barrier_semaphore()
    friends = [at_y(k) for k in range(1, NY)] + [at_x(i) for i in range(1, NX)]
    friends += [at_z(k) for k in range(1, NZ)]
    friends += [partner, beside(2), beside(-2)]
    for device in friends:
        pl.semaphore_signal(barrier, inc=1, device_id=device, device_id_type=MESH)

    ins[0].wait()
    coords = pts[...].astype(F32) * 0.25
    high, mid, low = parts_of(-0.5 * jnp.sum(coords * coords, axis=0, keepdims=True))
    rows = row_ids((16, LEAF))
    ones = jnp.where((rows < 3) | (rows == 14), 1.0, 0.0)
    tail = jnp.where(rows == 3, high, jnp.where(rows == 4, mid, jnp.where(rows == 5, low, ones)))
    near_pts[0, 0:FEAT, :] = coords.astype(BF16)
    near_pts[0, FEAT:TROWS, :] = tail.astype(BF16)
    near_pts[:, TROWS:, :] = jnp.zeros((5, LANES - TROWS, LEAF), BF16)
    sib_pts[TROWS:, :] = jnp.zeros((LANES - TROWS, SIB), BF16)

    ins[1].wait()
    picks = jnp.where(row_ids((LEAF, SK)) == skr[...], 1.0, 0.0).astype(BF16)
    skel_t[...] = jnp.dot(near_pts[0], picks, preferred_element_type=F32)

    ins[2].wait()
    ins[3].wait()
    charges = lax.dot_general(
        itp[...], near_mass[0], (((0,), (0,)), ((), ())), preferred_element_type=F32
    ).astype(BF16)
    sib_mass[0:SK, :] = charges

    ins[4].wait()
    ins[5].wait()
    mine = row_ids((SK, CSK)) + lax.rem(leaf, NY * NC) * SK
    picks = jnp.where(mine == clr[pl.ds(x, 1), :], 1.0, 0.0).astype(BF16)
    chosen = jnp.dot(skel_t[...].astype(BF16), picks, preferred_element_type=F32).T
    spread = lax.dot_general(
        cin[...], charges, (((0,), (0,)), ((), ())), preferred_element_type=F32
    )
    for b in range(NY * NC):
        c_all[b, :, 0:LANES] = chosen[b * PART:(b + 1) * PART]
        c_all[b, :, LANES:] = spread[b * PART:(b + 1) * PART]
    for yy in range(NY):
        c1_out[yy] = c_all[yy * NC + (1 - c)].astype(BF16)

    hot = jnp.where(row_ids((TROWS, SK)) == HOT + x * NC + c, 1.0, 0.0)
    sib_pts[0:TROWS, 0:SK] = (skel_t[0:TROWS, :] + hot).astype(BF16)

    ins[6].wait()
    flags = nfl[...].astype(F32)

    def flag_of(column):
        chosen = jnp.where(lane_ids(flags.shape) == column, flags, 0.0)
        return jnp.sum(chosen, axis=1, keepdims=True)

    def turned(block):
        return block.astype(F32).T.astype(BF16)

    rows = row_ids((16, SK))
    tail = jnp.where((rows >= 3) & (rows < 6), 1.0, 0.0)
    for j in range(3):
        tail = jnp.where(rows == j, skel_t[TAIL + 3 + j:TAIL + 4 + j, :], tail)
    listed = [flag_of(column) for column in range(5)]
    for j in range(5):
        tail = jnp.where(rows == 6 + j, listed[j], tail)
    tgt_in[0, 0:FEAT, :] = skel_t[0:FEAT, :].astype(BF16)
    tgt_in[0, FEAT:TROWS, :] = tail.astype(BF16)

    pl.semaphore_wait(barrier, len(friends))

    sent = []

    def go(copy):
        copy.start()
        sent.append(copy)
        return copy

    def sib_block(i):
        return sib_pts.at[0:TROWS, i * SK:(i + 1) * SK]

    def sib_rows(i):
        return sib_mass.at[i * SK:(i + 1) * SK]

    def pass_sibling(i):
        return [
            go(remote(sib_block(i), sib_block(NX + i), bp_s.at[0, i], bp_r.at[0, i], partner)),
            go(remote(sib_rows(i), sib_rows(NX + i), bp_s.at[1, i], bp_r.at[1, i], partner)),
        ]

    def near_copies(slot_from, slot_to, n, device):
        return [
            remote(
                near_pts.at[slot_from, 0:TROWS], near_pts.at[slot_to, 0:TROWS],
                f_s.at[0, n], f_r.at[0, n], device,
            ),
            remote(
                near_mass.at[slot_from], near_mass.at[slot_to], f_s.at[1, n], f_r.at[1, n], device
            ),
        ]

    f_partner = near_copies(0, 1, 0, partner)
    f_up = near_copies(0, 3, 1, beside(2))
    f_down = near_copies(0, 2, 2, beside(-2))
    f_last = near_copies(2 + c, 4, 3, partner)
    sent += f_partner + f_up + f_down + f_last

    def start_if(wanted, copies):
        @pl.when(wanted)
        def _():
            for copy in copies:
                copy.start()

    def pass_target(slot, by):
        after = (slot + by) % NY
        return go(remote(
            tgt_in.at[slot], tgt_in.at[after], a_s.at[after], a_r.at[after], at_y(by)
        ))

    ax = {1: pass_target(0, 1), 7: pass_target(0, -1)}
    c1 = go(remote(c1_out, c1_in, c1_s, c1_r, partner))
    bx = [
        [
            go(remote(sib_block(0), sib_block(i), bx_s.at[0, i], bx_r.at[0, i], at_x(i))),
            go(remote(sib_rows(0), sib_rows(i), bx_s.at[1, i], bx_r.at[1, i], at_x(i))),
        ]
        for i in range(1, NX)
    ]
    bp = pass_sibling(0)
    for copy in f_partner:
        copy.start()

    c1.wait_recv()
    for yy in range(NY):
        c2_out[yy] = (c_all[yy * NC + c] + c1_in[yy].astype(F32)).astype(BF16)
    order = (4, 3, 5, 2, 6, 1, 7)
    c2 = [
        go(remote(
            c2_out.at[lax.rem(y + k, NY)], c2_in.at[k], c2_s.at[k], c2_r.at[k], at_y(k)
        ))
        for k in order
    ]
    rows = row_ids((16, LEAF))
    tail = near_pts[0, FEAT:TROWS, :].astype(F32)
    ones = jnp.where((rows >= 3) & (rows < 6), 1.0, 0.0)
    tail = jnp.where(
        rows == 0, tail[3:4], jnp.where(rows == 1, tail[4:5], jnp.where(rows == 2, tail[5:6], ones))
    )
    near_tgt[...] = turned(jnp.concatenate(
        [near_pts[0, 0:FEAT, :].astype(F32), tail, jnp.zeros((LANES - TROWS, LEAF), F32)], axis=0
    ))

    def near_tile(slot_at, flag):
        gate = jnp.where(lane_ids((1, LANES)) == GATE, BIG * (1.0 - flag), 0.0).astype(BF16)
        exponent = jnp.dot(near_tgt[...] + gate, near_pts[slot_at], preferred_element_type=F32)
        return jnp.dot(
            jnp.exp(exponent).astype(BF16), near_mass[slot_at], preferred_element_type=F32
        )

    side = jnp.where(c == 0, 3, 1)
    near_columns = (2, side, 4, 0, 4 - side)

    def near_step(s):
        near_acc[...] += near_tile(s, flag_of(near_columns[s]))

    near_acc[...] = near_tile(0, listed[2])

    ax[1].wait_recv()
    ax[2] = pass_target(1, 1)
    ax[7].wait_recv()
    ax[6] = pass_target(7, -1)
    wrap_up = remote(near_pts.at[0, 0:TROWS], wrap, w_s, w_r, at_y(1))
    wrap_down = remote(near_pts.at[0, 0:TROWS], wrap, w_s, w_r, at_y(-1))
    start_if(y == NY - 1, f_up[1:])
    start_if(y == 0, f_down[1:])
    def relay_sibling(i):
        for copy in bx[i - 1]:
            copy.wait_recv()
        return pass_sibling(i)

    bp += relay_sibling(1) + relay_sibling(3)
    ax[2].wait_recv()
    ax[3] = pass_target(2, 1)
    ax[6].wait_recv()
    ax[5] = pass_target(6, -1)
    start_if(y == NY - 1, [wrap_up])
    start_if(y == 0, [wrap_down])
    part = c_all[y * NC + c] + c1_in[y].astype(F32)
    for copy, k in zip(c2, order):
        copy.wait_recv()
        part = part + c2_in[k].astype(F32)
    d_out[...] = part.astype(BF16)
    ring = (1, 7, 2, 6, 3, 5, 4)
    groups = ((0, 4), (4, 7))

    def far_rows(half, i, first, last):
        start = (half * NX + i) * (NZ - 1) * PART
        return far.at[start + first * PART:start + last * PART]

    dz = [
        go(remote(d_out, far_rows(0, 0, n, n + 1), dz_s.at[n], dz_r.at[n], at_z(k)))
        for n, k in enumerate(ring)
    ]
    dx, dp = {}, []

    def pass_far(i, g):
        return go(remote(
            far_rows(0, i, *groups[g]), far_rows(1, i, *groups[g]),
            dp_s.at[g, i], dp_r.at[g, i], partner,
        ))

    def spread_far(g):
        for n in range(*groups[g]):
            dz[n].wait_recv()
        for i in (2, 1, 3):
            dx[g, i] = go(remote(
                far_rows(0, 0, *groups[g]), far_rows(0, i, *groups[g]),
                dx_s.at[g, i], dx_r.at[g, i], at_x(i),
            ))
        dp.append(pass_far(0, g))

    def relay_far(g):
        for i in (1, 3, 2):
            dx[g, i].wait_recv()
            dp.append(pass_far(i, g))

    bp += relay_sibling(2)
    for copy in bp:
        copy.wait_recv()
    slots = (4, 2, 6, 5, 3, 7, 1, 0)
    pad = jnp.zeros((LANES - TROWS, SK), F32)

    def sibling_step(p):
        at = slice(p * 2 * SK, (p + 1) * 2 * SK)
        for h in range(2):
            k = slots[p * 2 + h]
            tail = tgt_in[k, FEAT:TROWS, :].astype(F32)
            rows = row_ids((16, SK))
            slot = rows - 6
            other = lax.shift_right_logical(slot, 1) * (NY * NC) + y * NC + (slot & 1)
            column = other - place(x, lax.rem(y - k + NY, NY), c) + 2
            hidden = jnp.zeros((16, SK), F32)
            for j in range(5):
                hidden = jnp.where(column == j, tail[6 + j:7 + j, :], hidden)
            hidden = jnp.where(slot < NX * NC, BIG * hidden, 0.0)
            tail = jnp.where(slot < 0, tail, hidden)
            block = jnp.concatenate([tgt_in[k, 0:FEAT, :].astype(F32), tail, pad], axis=0)
            tgt[(p * 2 + h) * SK:(p * 2 + h + 1) * SK, :] = turned(block)
        exponent = jnp.dot(tgt[at, :], sib_pts[...], preferred_element_type=F32)
        acc[at, :] = jnp.dot(
            jnp.exp(exponent).astype(BF16), sib_mass[...], preferred_element_type=F32
        )

    sibling_step(3)
    spread_far(0)
    ax[3].wait_recv()
    ax[4] = pass_target(3, 1)
    start_if(y < NY - 1, f_up)
    start_if(y > 0, f_down)
    sibling_step(2)
    spread_far(1)
    ax[5].wait_recv()
    sibling_step(1)
    relay_far(0)
    @pl.when(y == 0)
    def _():
        wrap_up.wait_recv()
        remote(wrap, near_pts.at[3, 0:TROWS], f_s.at[0, 2], f_r.at[0, 1], at_x(1)).start()

    @pl.when(y == NY - 1)
    def _():
        wrap_down.wait_recv()
        remote(wrap, near_pts.at[2, 0:TROWS], f_s.at[0, 1], f_r.at[0, 2], at_x(NX - 1)).start()

    ax[4].wait_recv()
    sibling_step(0)
    relay_far(1)

    for copy in dp:
        copy.wait_recv()

    e_from = {3: 4, 1: 2, 7: 6}
    e_to = {4: -1, 2: -1, 6: 1, 5: 3, 3: -3, 7: 1, 1: -1}
    e_land = {4: 4, 2: 2, 6: 6, 5: 5, 3: 3, 7: 7, 1: 1}
    ex = {
        k: remote(e_out.at[k], e_in.at[e_land[k]], e_s.at[k], e_r.at[k], at_y(by))
        for k, by in e_to.items()
    }
    sent += list(ex.values())

    def distant_step(p):
        at = slice(p * 2 * SK, (p + 1) * 2 * SK)
        acc[at, :] = acc[at, :] + tile_product(tgt[at, :], far[:, 0:LANES], far[:, LANES:])

    def hand_on(k):
        row = slots.index(k) * SK
        block = acc[row:row + SK, :]
        if k in e_from:
            ex[e_from[k]].wait_recv()
            block = block + e_in[e_from[k]].astype(F32)
        e_out[k] = block.astype(BF16)
        ex[k].start()

    distant_step(0)
    hand_on(4)
    hand_on(2)
    distant_step(1)
    hand_on(6)
    hand_on(5)
    for copy in f_partner:
        copy.wait_recv()
    near_step(1)
    distant_step(2)
    hand_on(3)
    hand_on(7)
    distant_step(3)
    hand_on(1)
    for copy in f_up + f_down:
        copy.wait_recv()
    for copy in f_last:
        copy.start()
    near_step(2)
    near_step(3)
    for copy in f_last:
        copy.wait_recv()
    near_step(4)

    row = slots.index(0) * SK
    phi = acc[row:row + SK, :]
    for k in (1, 7, 3, 5):
        ex[k].wait_recv()
        phi = phi + e_in[k].astype(F32)
    out_ref[...] = (
        near_acc[...] + jnp.dot(itp[...], phi.astype(BF16), preferred_element_type=F32)
    ).astype(BF16)

    for copy in sent:
        copy.wait_send()

    @pl.when((y == 0) | (y == NY - 1))
    def _():
        wrap_up.wait_send()


def on_device(points, weights, interp, cluster_interp, skeleton_rows, near_flags, cluster_rows):
    vmem, dma = pltpu.VMEM, pltpu.SemaphoreType.DMA
    return pl.pallas_call(
        kernel,
        out_shape=pltpu.VMEM(weights.shape, BF16),
        in_specs=[pl.BlockSpec(memory_space=pl.ANY)] * 7,
        out_specs=pl.BlockSpec(memory_space=pltpu.VMEM),
        scratch_shapes=[
            vmem((FEAT, LEAF), BF16),
            vmem((LEAF, SK), BF16),
            vmem((SK, CSK), BF16),
            vmem((1, SK), jnp.int32),
            vmem((1, 5), jnp.int32),
            vmem((NX, CSK), jnp.int32),
            vmem((5, LANES, LEAF), BF16),
            vmem((5, LEAF, LANES), BF16),
            vmem((LEAF, LANES), BF16),
            vmem((LEAF, LANES), F32),
            vmem((LANES, SK), F32),
            vmem((NY, TROWS, SK), BF16),
            vmem((NY * SK, LANES), BF16),
            vmem((LANES, SIB), BF16),
            vmem((SIB, LANES), BF16),
            vmem((DIST, 2 * LANES), BF16),
            vmem((NY * SK, LANES), F32),
            vmem((NY * NC, PART, 2 * LANES), F32),
            vmem((NY, PART, 2 * LANES), BF16),
            vmem((NY, PART, 2 * LANES), BF16),
            vmem((NY, PART, 2 * LANES), BF16),
            vmem((NY, PART, 2 * LANES), BF16),
            vmem((PART, 2 * LANES), BF16),
            vmem((NY, SK, LANES), BF16),
            vmem((NY, SK, LANES), BF16),
            vmem((TROWS, LEAF), BF16),
            dma((7,)),
            dma, dma,
            dma((NY,)), dma((NY,)),
            dma((NY,)), dma((NY,)),
            dma((2, NX)), dma((2, NX)),
            dma((2, NX)), dma((2, NX)),
            dma((NZ - 1,)), dma((NZ - 1,)),
            dma((2, NX)), dma((2, NX)),
            dma((2, NX)), dma((2, NX)),
            dma((2, 4)), dma((2, 4)),
            dma((NY,)), dma((NY,)),
            dma, dma,
        ],
        compiler_params=pltpu.CompilerParams(
            collective_id=0, has_side_effects=True, vmem_limit_bytes=60 << 20
        ),
        name="hier",
    )(points.T, weights, interp, cluster_interp, skeleton_rows, near_flags, cluster_rows)


def solution(mesh):
    placed = P(("group", "leaf"), None)
    return jax.shard_map(
        on_device,
        mesh=mesh,
        in_specs=(placed,) * 6 + (P("group", None),),
        out_specs=placed,
        check_vma=False,
    )
```

```python
import jax
import jax.numpy as jnp
from jax import lax
from jax.experimental import pallas as pl
from jax.experimental.pallas import tpu as pltpu
from jax.sharding import PartitionSpec as P

MESH = pl.DeviceIdType.MESH
F32, BF16 = jnp.float32, jnp.bfloat16

FEAT = 64
LANES = 128
LEAF = 1024
SK = 256
CSK = 512
NX, NY, NZ, NC = 4, 8, 8, 2
TAIL = 64
HOT = TAIL + 6
GATE = TAIL + 14
TROWS = 80
BIG = -30000.0
SIB = NX * NC * SK
PART = CSK // (NY * NC)
HALF = NX * (NZ - 1) * PART
DIST = NC * HALF


def row_ids(shape):
    return lax.broadcasted_iota(jnp.int32, shape, 0)


def lane_ids(shape):
    return lax.broadcasted_iota(jnp.int32, shape, 1)


def parts_of(norm):
    high = norm.astype(BF16).astype(F32)
    rest = norm - high
    mid = rest.astype(BF16).astype(F32)
    return high, mid, (rest - mid).astype(BF16).astype(F32)


def tile_product(targets, sources, mass):
    exponent = lax.dot_general(
        targets, sources, (((1,), (1,)), ((), ())), preferred_element_type=F32
    )
    return jnp.dot(jnp.exp(exponent).astype(BF16), mass, preferred_element_type=F32)


def kernel(
    pts_h, wts_h, itp_h, cin_h, skr_h, nfl_h, clr_h, out_ref,
    pts, itp, cin, skr, nfl, clr,
    near_pts, near_mass, near_tgt, near_acc,
    skel_t, tgt_in, tgt, sib_pts, sib_mass, far, acc,
    c_all, c1_out, c1_in, c2_out, c2_in, d_out,
    e_out, e_in, wrap,
    in_sem, c1_s, c1_r, c2_s, c2_r, a_s, a_r, bx_s, bx_r, bp_s, bp_r,
    dz_s, dz_r, dx_s, dx_r, dp_s, dp_r, f_s, f_r, e_s, e_r, w_s, w_r,
):
    z = lax.axis_index("group")
    leaf = lax.axis_index("leaf")
    x = lax.div(leaf, NY * NC)
    y = lax.rem(lax.div(leaf, NC), NY)
    c = lax.rem(leaf, NC)

    def place(xx, yy, cc):
        return xx * (NY * NC) + yy * NC + cc

    def at_y(k):
        return (z, place(x, lax.rem(y + k + NY, NY), c))

    def at_x(i):
        return (z, place(lax.rem(x + i, NX), y, c))

    def at_z(k):
        return (lax.rem(z + k, NZ), leaf)

    def beside(step):
        return (z, lax.rem(leaf + step + NX * NY * NC, NX * NY * NC))

    partner = (z, place(x, y, 1 - c))

    def remote(source, target, send, recv, device):
        return pltpu.make_async_remote_copy(
            src_ref=source, dst_ref=target, send_sem=send, recv_sem=recv,
            device_id=device, device_id_type=MESH,
        )

    def all_landed(region, sem):
        pltpu.make_async_copy(region, region, sem).wait()

    ins = [
        pltpu.make_async_copy(pts_h, pts, in_sem.at[0]),
        pltpu.make_async_copy(skr_h, skr, in_sem.at[1]),
        pltpu.make_async_copy(wts_h, near_mass.at[0], in_sem.at[2]),
        pltpu.make_async_copy(itp_h, itp, in_sem.at[3]),
        pltpu.make_async_copy(cin_h, cin, in_sem.at[4]),
        pltpu.make_async_copy(clr_h, clr, in_sem.at[5]),
        pltpu.make_async_copy(nfl_h, nfl, in_sem.at[6]),
    ]
    for copy in ins:
        copy.start()

    barrier = pltpu.get_barrier_semaphore()
    friends = [at_y(k) for k in range(1, NY)] + [at_x(i) for i in range(1, NX)]
    friends += [at_z(k) for k in range(1, NZ)]
    friends += [partner, beside(2), beside(-2)]
    for device in friends:
        pl.semaphore_signal(barrier, inc=1, device_id=device, device_id_type=MESH)

    ins[0].wait()
    coords = pts[...].astype(F32) * 0.25
    high, mid, low = parts_of(-0.5 * jnp.sum(coords * coords, axis=0, keepdims=True))
    rows = row_ids((16, LEAF))
    ones = jnp.where((rows < 3) | (rows == 14), 1.0, 0.0)
    tail = jnp.where(rows == 3, high, jnp.where(rows == 4, mid, jnp.where(rows == 5, low, ones)))
    near_pts[0, 0:FEAT, :] = coords.astype(BF16)
    near_pts[0, FEAT:TROWS, :] = tail.astype(BF16)
    near_pts[:, TROWS:, :] = jnp.zeros((5, LANES - TROWS, LEAF), BF16)
    sib_pts[TROWS:, :] = jnp.zeros((LANES - TROWS, SIB), BF16)

    ins[1].wait()
    picks = jnp.where(row_ids((LEAF, SK)) == skr[...], 1.0, 0.0).astype(BF16)
    skel_t[...] = jnp.dot(near_pts[0], picks, preferred_element_type=F32)

    ins[2].wait()
    ins[3].wait()
    charges = lax.dot_general(
        itp[...], near_mass[0], (((0,), (0,)), ((), ())), preferred_element_type=F32
    ).astype(BF16)
    sib_mass[0:SK, :] = charges

    ins[4].wait()
    ins[5].wait()
    mine = row_ids((SK, CSK)) + lax.rem(leaf, NY * NC) * SK
    picks = jnp.where(mine == clr[pl.ds(x, 1), :], 1.0, 0.0).astype(BF16)
    chosen = jnp.dot(skel_t[...].astype(BF16), picks, preferred_element_type=F32).T
    spread = lax.dot_general(
        cin[...], charges, (((0,), (0,)), ((), ())), preferred_element_type=F32
    )
    for b in range(NY * NC):
        c_all[b, :, 0:LANES] = chosen[b * PART:(b + 1) * PART]
        c_all[b, :, LANES:] = spread[b * PART:(b + 1) * PART]
    for yy in range(NY):
        c1_out[yy] = c_all[yy * NC + (1 - c)].astype(BF16)

    hot = jnp.where(row_ids((TROWS, SK)) == HOT + x * NC + c, 1.0, 0.0)
    sib_pts[0:TROWS, 0:SK] = (skel_t[0:TROWS, :] + hot).astype(BF16)

    ins[6].wait()
    flags = nfl[...].astype(F32)

    def flag_of(column):
        chosen = jnp.where(lane_ids(flags.shape) == column, flags, 0.0)
        return jnp.sum(chosen, axis=1, keepdims=True)

    def turned(block):
        return block.astype(F32).T.astype(BF16)

    rows = row_ids((16, SK))
    tail = jnp.where((rows >= 3) & (rows < 6), 1.0, 0.0)
    for j in range(3):
        tail = jnp.where(rows == j, skel_t[TAIL + 3 + j:TAIL + 4 + j, :], tail)
    listed = [flag_of(column) for column in range(5)]
    for j in range(5):
        tail = jnp.where(rows == 6 + j, listed[j], tail)
    tgt_in[0, 0:FEAT, :] = skel_t[0:FEAT, :].astype(BF16)
    tgt_in[0, FEAT:TROWS, :] = tail.astype(BF16)

    pl.semaphore_wait(barrier, len(friends))

    def go(copy):
        copy.start()
        return copy

    def sib_block(i):
        return sib_pts.at[0:TROWS, i * SK:(i + 1) * SK]

    def sib_rows(i):
        return sib_mass.at[i * SK:(i + 1) * SK]

    def pass_sibling(i):
        return [
            go(remote(sib_block(i), sib_block(NX + i), bp_s.at[0], bp_r.at[0], partner)),
            go(remote(sib_rows(i), sib_rows(NX + i), bp_s.at[1], bp_r.at[1], partner)),
        ]

    def near_copies(slot_from, slot_to, n, device):
        return [
            remote(
                near_pts.at[slot_from, 0:TROWS], near_pts.at[slot_to, 0:TROWS],
                f_s.at[0], f_r.at[0, n], device,
            ),
        ] + [
            remote(
                near_mass.at[slot_from, h * LEAF // 2:(h + 1) * LEAF // 2],
                near_mass.at[slot_to, h * LEAF // 2:(h + 1) * LEAF // 2],
                f_s.at[1], f_r.at[1, n], device,
            )
            for h in range(2)
        ]

    f_partner = near_copies(0, 1, 0, partner)
    f_up = near_copies(0, 3, 1, beside(2))
    f_down = near_copies(0, 2, 2, beside(-2))
    f_last = near_copies(2 + c, 4, 3, partner)
    near_slot = (1, 3, 2, 4)

    def near_landed(n):
        all_landed(near_pts.at[near_slot[n], 0:TROWS], f_r.at[0, n])
        all_landed(near_mass.at[near_slot[n]], f_r.at[1, n])

    def start_if(wanted, copies):
        @pl.when(wanted)
        def _():
            for copy in copies:
                copy.start()

    def pass_target(slot, by):
        after = (slot + by) % NY
        return go(remote(
            tgt_in.at[slot], tgt_in.at[after], a_s, a_r.at[after], at_y(by)
        ))

    ax = {1: pass_target(0, 1), 7: pass_target(0, -1)}
    c1 = go(remote(c1_out, c1_in, c1_s, c1_r, partner))
    bx = [
        [
            go(remote(sib_block(0), sib_block(i), bx_s.at[0], bx_r.at[0, i], at_x(i))),
            go(remote(sib_rows(0), sib_rows(i), bx_s.at[1], bx_r.at[1, i], at_x(i))),
        ]
        for i in range(1, NX)
    ]
    pass_sibling(0)
    for copy in f_partner:
        copy.start()

    c1.wait_recv()
    for yy in range(NY):
        c2_out[yy] = (c_all[yy * NC + c] + c1_in[yy].astype(F32)).astype(BF16)
    order = (4, 3, 5, 2, 6, 1, 7)
    for k in order:
        go(remote(c2_out.at[lax.rem(y + k, NY)], c2_in.at[k], c2_s, c2_r, at_y(k)))
    rows = row_ids((16, LEAF))
    tail = near_pts[0, FEAT:TROWS, :].astype(F32)
    ones = jnp.where((rows >= 3) & (rows < 6), 1.0, 0.0)
    tail = jnp.where(
        rows == 0, tail[3:4], jnp.where(rows == 1, tail[4:5], jnp.where(rows == 2, tail[5:6], ones))
    )
    near_tgt[...] = turned(jnp.concatenate(
        [near_pts[0, 0:FEAT, :].astype(F32), tail, jnp.zeros((LANES - TROWS, LEAF), F32)], axis=0
    ))

    def near_tile(slot_at, flag):
        gate = jnp.where(lane_ids((1, LANES)) == GATE, BIG * (1.0 - flag), 0.0).astype(BF16)
        exponent = jnp.dot(near_tgt[...] + gate, near_pts[slot_at], preferred_element_type=F32)
        return jnp.dot(
            jnp.exp(exponent).astype(BF16), near_mass[slot_at], preferred_element_type=F32
        )

    side = jnp.where(c == 0, 3, 1)
    near_columns = (2, side, 4, 0, 4 - side)

    def near_step(s):
        near_acc[...] += near_tile(s, flag_of(near_columns[s]))

    near_acc[...] = near_tile(0, listed[2])

    near_landed(0)
    near_step(1)
    ax[1].wait_recv()
    ax[2] = pass_target(1, 1)
    ax[7].wait_recv()
    ax[6] = pass_target(7, -1)
    wrap_up = remote(near_pts.at[0, 0:TROWS], wrap, w_s, w_r, at_y(1))
    wrap_down = remote(near_pts.at[0, 0:TROWS], wrap, w_s, w_r, at_y(-1))
    start_if(y == NY - 1, f_up[1:2])
    start_if(y == 0, f_down[1:2])
    def relay_sibling(i):
        for copy in bx[i - 1]:
            copy.wait_recv()
        pass_sibling(i)

    relay_sibling(3)
    relay_sibling(1)
    part = c_all[y * NC + c] + c1_in[y].astype(F32)
    all_landed(c2_in.at[1:], c2_r)
    for k in order:
        part = part + c2_in[k].astype(F32)
    d_out[...] = part.astype(BF16)
    ring = (1, 7, 2, 6, 3, 5, 4)
    groups = ((0, 4), (4, 7))

    def far_rows(half, g, i, first=0, last=None, count=1):
        blocks = groups[g][1] - groups[g][0]
        start = half * HALF + (groups[g][0] * NX + i * blocks) * PART
        last = blocks * count if last is None else last
        return far.at[start + first * PART:start + last * PART]

    for n, k in enumerate(ring):
        g = 0 if n < groups[0][1] else 1
        at = n - groups[g][0]
        go(remote(d_out, far_rows(0, g, 0, at, at + 1), dz_s, dz_r.at[g], at_z(k)))

    def pass_far(g, i, count):
        go(remote(
            far_rows(0, g, i, count=count), far_rows(1, g, i, count=count), dp_s, dp_r, partner
        ))

    def spread_far(g):
        all_landed(far_rows(0, g, 0), dz_r.at[g])
        for i in (2, 1, 3):
            go(remote(far_rows(0, g, 0), far_rows(0, g, i), dx_s, dx_r.at[g], at_x(i)))
        pass_far(g, 0, 1)

    def relay_far(g):
        all_landed(far_rows(0, g, 1, count=NX - 1), dx_r.at[g])
        pass_far(g, 1, NX - 1)

    ax[2].wait_recv()
    ax[3] = pass_target(2, 1)
    ax[6].wait_recv()
    ax[5] = pass_target(6, -1)
    relay_sibling(2)
    all_landed(sib_pts.at[0:TROWS, NX * SK:], bp_r.at[0])
    all_landed(sib_mass.at[NX * SK:], bp_r.at[1])
    slots = (4, 6, 2, 5, 3, 7, 1, 0)
    pad = jnp.zeros((LANES - TROWS, SK), F32)

    def sibling_step(p):
        at = slice(p * 2 * SK, (p + 1) * 2 * SK)
        for h in range(2):
            k = slots[p * 2 + h]
            tail = tgt_in[k, FEAT:TROWS, :].astype(F32)
            rows = row_ids((16, SK))
            slot = rows - 6
            other = lax.shift_right_logical(slot, 1) * (NY * NC) + y * NC + (slot & 1)
            column = other - place(x, lax.rem(y - k + NY, NY), c) + 2
            hidden = jnp.zeros((16, SK), F32)
            for j in range(5):
                hidden = jnp.where(column == j, tail[6 + j:7 + j, :], hidden)
            hidden = jnp.where(slot < NX * NC, BIG * hidden, 0.0)
            tail = jnp.where(slot < 0, tail, hidden)
            block = jnp.concatenate([tgt_in[k, 0:FEAT, :].astype(F32), tail, pad], axis=0)
            tgt[(p * 2 + h) * SK:(p * 2 + h + 1) * SK, :] = turned(block)
        exponent = jnp.dot(tgt[at, :], sib_pts[...], preferred_element_type=F32)
        acc[at, :] = jnp.dot(
            jnp.exp(exponent).astype(BF16), sib_mass[...], preferred_element_type=F32
        )

    sibling_step(3)
    spread_far(0)
    ax[3].wait_recv()
    ax[4] = pass_target(3, 1)
    start_if(y == NY - 1, [wrap_up])
    start_if(y == 0, [wrap_down])
    start_if(y < NY - 1, f_up)
    start_if(y > 0, f_down)
    sibling_step(2)
    spread_far(1)
    ax[5].wait_recv()
    sibling_step(1)
    relay_far(0)
    ax[4].wait_recv()
    sibling_step(0)
    @pl.when(y == 0)
    def _():
        wrap_up.wait_recv()
        remote(wrap, near_pts.at[3, 0:TROWS], f_s.at[0], f_r.at[0, 1], at_x(1)).start()

    @pl.when(y == NY - 1)
    def _():
        wrap_down.wait_recv()
        remote(wrap, near_pts.at[2, 0:TROWS], f_s.at[0], f_r.at[0, 2], at_x(NX - 1)).start()

    relay_far(1)

    start_if(y == NY - 1, f_up[2:])
    start_if(y == 0, f_down[2:])
    e_from = {3: 4, 1: 2, 7: 6}
    e_to = {4: -1, 2: -1, 6: 1, 5: 3, 3: -3, 7: 1, 1: -1}
    e_land = {4: 4, 2: 5, 6: 6, 5: 0, 3: 1, 7: 2, 1: 3}
    e_sem = {4: 1, 2: 2, 6: 3, 5: 0, 3: 0, 7: 0, 1: 0}
    ex = {
        k: remote(e_out.at[k], e_in.at[e_land[k]], e_s, e_r.at[e_sem[k]], at_y(by))
        for k, by in e_to.items()
    }

    def distant_step(p, first=0, last=DIST):
        at = slice(p * 2 * SK, (p + 1) * 2 * SK)
        acc[at, :] = acc[at, :] + tile_product(
            tgt[at, :], far[first:last, 0:LANES], far[first:last, LANES:]
        )

    def hand_on(k):
        row = slots.index(k) * SK
        block = acc[row:row + SK, :]
        if k in e_from:
            ex[e_from[k]].wait_recv()
            block = block + e_in[e_land[e_from[k]]].astype(F32)
        e_out[k] = block.astype(BF16)
        ex[k].start()

    distant_step(0, 0, HALF)
    all_landed(far.at[HALF:], dp_r)
    distant_step(0, HALF, DIST)
    hand_on(4)
    hand_on(6)
    distant_step(1)
    hand_on(5)
    hand_on(2)
    distant_step(2)
    hand_on(3)
    hand_on(7)
    distant_step(3)
    hand_on(1)
    near_landed(1)
    near_landed(2)
    for copy in f_last:
        copy.start()
    near_step(2)
    near_step(3)
    near_landed(3)
    near_step(4)

    row = slots.index(0) * SK
    phi = acc[row:row + SK, :]
    all_landed(e_in.at[0:4], e_r.at[0])
    for n in range(4):
        phi = phi + e_in[n].astype(F32)
    out_ref[...] = (
        near_acc[...] + jnp.dot(itp[...], phi.astype(BF16), preferred_element_type=F32)
    ).astype(BF16)

    c1.wait_send()
    all_landed(c2_out.at[1:], c2_s)
    all_landed(tgt_in.at[1:], a_s)
    all_landed(sib_pts.at[0:TROWS, SK:NX * SK], bx_s.at[0])
    all_landed(sib_mass.at[SK:NX * SK], bx_s.at[1])
    all_landed(sib_pts.at[0:TROWS, 0:NX * SK], bp_s.at[0])
    all_landed(sib_mass.at[0:NX * SK], bp_s.at[1])
    all_landed(far.at[0:(NZ - 1) * PART], dz_s)
    all_landed(far.at[0:(NX - 1) * (NZ - 1) * PART], dx_s)
    all_landed(far.at[0:HALF], dp_s)
    all_landed(near_pts.at[1:, 0:TROWS], f_s.at[0])
    all_landed(near_mass.at[1:], f_s.at[1])
    all_landed(e_out.at[1:], e_s)

    @pl.when((y == 0) | (y == NY - 1))
    def _():
        wrap_up.wait_send()


def on_device(points, weights, interp, cluster_interp, skeleton_rows, near_flags, cluster_rows):
    vmem, dma = pltpu.VMEM, pltpu.SemaphoreType.DMA
    return pl.pallas_call(
        kernel,
        out_shape=pltpu.VMEM(weights.shape, BF16),
        in_specs=[pl.BlockSpec(memory_space=pl.ANY)] * 7,
        out_specs=pl.BlockSpec(memory_space=pltpu.VMEM),
        scratch_shapes=[
            vmem((FEAT, LEAF), BF16),
            vmem((LEAF, SK), BF16),
            vmem((SK, CSK), BF16),
            vmem((1, SK), jnp.int32),
            vmem((1, 5), jnp.int32),
            vmem((NX, CSK), jnp.int32),
            vmem((5, LANES, LEAF), BF16),
            vmem((5, LEAF, LANES), BF16),
            vmem((LEAF, LANES), BF16),
            vmem((LEAF, LANES), F32),
            vmem((LANES, SK), F32),
            vmem((NY, TROWS, SK), BF16),
            vmem((NY * SK, LANES), BF16),
            vmem((LANES, SIB), BF16),
            vmem((SIB, LANES), BF16),
            vmem((DIST, 2 * LANES), BF16),
            vmem((NY * SK, LANES), F32),
            vmem((NY * NC, PART, 2 * LANES), F32),
            vmem((NY, PART, 2 * LANES), BF16),
            vmem((NY, PART, 2 * LANES), BF16),
            vmem((NY, PART, 2 * LANES), BF16),
            vmem((NY, PART, 2 * LANES), BF16),
            vmem((PART, 2 * LANES), BF16),
            vmem((NY, SK, LANES), BF16),
            vmem((NY, SK, LANES), BF16),
            vmem((TROWS, LEAF), BF16),
            dma((7,)),
            dma, dma,
            dma, dma,
            dma, dma((NY,)),
            dma((2,)), dma((2, NX)),
            dma((2,)), dma((2,)),
            dma, dma((2,)),
            dma, dma((2,)),
            dma, dma,
            dma((2,)), dma((2, 4)),
            dma, dma((4,)),
            dma, dma,
        ],
        compiler_params=pltpu.CompilerParams(
            collective_id=0, has_side_effects=True, vmem_limit_bytes=60 << 20
        ),
        name="hier",
    )(points.T, weights, interp, cluster_interp, skeleton_rows, near_flags, cluster_rows)


def solution(mesh):
    placed = P(("group", "leaf"), None)
    return jax.shard_map(
        on_device,
        mesh=mesh,
        in_specs=(placed,) * 6 + (P("group", None),),
        out_specs=placed,
        check_vma=False,
    )
```

```python
import jax
import jax.numpy as jnp
from jax import lax
from jax.experimental import pallas as pl
from jax.experimental.pallas import tpu as pltpu
from jax.sharding import PartitionSpec as P

MESH = pl.DeviceIdType.MESH
F32, BF16 = jnp.float32, jnp.bfloat16

FEAT = 64
LANES = 128
LEAF = 1024
SK = 256
CSK = 512
NX, NY, NZ, NC = 4, 8, 8, 2
TAIL = 64
HOT = TAIL + 6
GATE = TAIL + 14
TROWS = 80
BIG = -30000.0
SIB = NX * NC * SK
PART = CSK // (NY * NC)
HALF = NX * (NZ - 1) * PART
DIST = NC * HALF


def row_ids(shape):
    return lax.broadcasted_iota(jnp.int32, shape, 0)


def lane_ids(shape):
    return lax.broadcasted_iota(jnp.int32, shape, 1)


def parts_of(norm):
    high = norm.astype(BF16).astype(F32)
    rest = norm - high
    mid = rest.astype(BF16).astype(F32)
    return high, mid, (rest - mid).astype(BF16).astype(F32)


def tile_product(targets, sources, mass):
    exponent = lax.dot_general(
        targets, sources, (((1,), (1,)), ((), ())), preferred_element_type=F32
    )
    return jnp.dot(jnp.exp(exponent).astype(BF16), mass, preferred_element_type=F32)


def kernel(
    pts_h, wts_h, itp_h, cin_h, skr_h, nfl_h, clr_h, out_ref,
    pts, itp, cin, skr, nfl, clr,
    near_pts, near_mass, near_tgt, near_acc,
    skel_t, tgt_in, tgt, sib_pts, sib_mass, far, acc,
    c_all, c1_out, c1_in, c2_out, c2_in, d_out,
    e_out, e_in, wrap,
    in_sem, c1_s, c1_r, c2_s, c2_r, a_s, a_r, bx_s, bx_r, bp_s, bp_r,
    dz_s, dz_r, dx_s, dx_r, dp_s, dp_r, f_s, f_r, e_s, e_r, w_s, w_r, ready,
):
    z = lax.axis_index("group")
    leaf = lax.axis_index("leaf")
    x = lax.div(leaf, NY * NC)
    y = lax.rem(lax.div(leaf, NC), NY)
    c = lax.rem(leaf, NC)

    def place(xx, yy, cc):
        return xx * (NY * NC) + yy * NC + cc

    def at_y(k):
        return (z, place(x, lax.rem(y + k + NY, NY), c))

    def at_x(i):
        return (z, place(lax.rem(x + i, NX), y, c))

    def at_z(k):
        return (lax.rem(z + k, NZ), leaf)

    def beside(step):
        return (z, lax.rem(leaf + step + NX * NY * NC, NX * NY * NC))

    partner = (z, place(x, y, 1 - c))

    def remote(source, target, send, recv, device):
        return pltpu.make_async_remote_copy(
            src_ref=source, dst_ref=target, send_sem=send, recv_sem=recv,
            device_id=device, device_id_type=MESH,
        )

    def all_landed(region, sem):
        pltpu.make_async_copy(region, region, sem).wait()

    ins = [
        pltpu.make_async_copy(pts_h, pts, in_sem.at[0]),
        pltpu.make_async_copy(skr_h, skr, in_sem.at[1]),
        pltpu.make_async_copy(wts_h, near_mass.at[0], in_sem.at[2]),
        pltpu.make_async_copy(itp_h, itp, in_sem.at[3]),
        pltpu.make_async_copy(cin_h, cin, in_sem.at[4]),
        pltpu.make_async_copy(clr_h, clr, in_sem.at[5]),
        pltpu.make_async_copy(nfl_h, nfl, in_sem.at[6]),
    ]
    for copy in ins:
        copy.start()

    barrier = pltpu.get_barrier_semaphore()
    friends = [at_y(k) for k in range(1, NY)] + [at_x(i) for i in range(1, NX)]
    friends += [partner, beside(2), beside(-2)]
    for device in friends:
        pl.semaphore_signal(barrier, inc=1, device_id=device, device_id_type=MESH)

    def greet(other, carry):
        pl.semaphore_signal(barrier, inc=1, device_id=(other, leaf), device_id_type=MESH)
        return carry

    lax.fori_loop(z + 1, NZ, greet, 0)

    ins[0].wait()
    coords = pts[...].astype(F32) * 0.25
    high, mid, low = parts_of(-0.5 * jnp.sum(coords * coords, axis=0, keepdims=True))
    rows = row_ids((16, LEAF))
    ones = jnp.where((rows < 3) | (rows == 14), 1.0, 0.0)
    tail = jnp.where(rows == 3, high, jnp.where(rows == 4, mid, jnp.where(rows == 5, low, ones)))
    near_pts[0, 0:FEAT, :] = coords.astype(BF16)
    near_pts[0, FEAT:TROWS, :] = tail.astype(BF16)
    near_pts[:, TROWS:, :] = jnp.zeros((5, LANES - TROWS, LEAF), BF16)
    sib_pts[TROWS:, :] = jnp.zeros((LANES - TROWS, SIB), BF16)

    ins[1].wait()
    picks = jnp.where(row_ids((LEAF, SK)) == skr[...], 1.0, 0.0).astype(BF16)
    skel_t[...] = jnp.dot(near_pts[0], picks, preferred_element_type=F32)

    ins[2].wait()
    ins[3].wait()
    charges = lax.dot_general(
        itp[...], near_mass[0], (((0,), (0,)), ((), ())), preferred_element_type=F32
    ).astype(BF16)
    sib_mass[0:SK, :] = charges

    ins[4].wait()
    ins[5].wait()
    mine = row_ids((SK, CSK)) + lax.rem(leaf, NY * NC) * SK
    picks = jnp.where(mine == clr[pl.ds(x, 1), :], 1.0, 0.0).astype(BF16)
    chosen = jnp.dot(skel_t[...].astype(BF16), picks, preferred_element_type=F32).T
    spread = lax.dot_general(
        cin[...], charges, (((0,), (0,)), ((), ())), preferred_element_type=F32
    )
    for b in range(NY * NC):
        c_all[b, :, 0:LANES] = chosen[b * PART:(b + 1) * PART]
        c_all[b, :, LANES:] = spread[b * PART:(b + 1) * PART]
    for yy in range(NY):
        c1_out[yy] = c_all[yy * NC + (1 - c)].astype(BF16)

    hot = jnp.where(row_ids((TROWS, SK)) == HOT + x * NC + c, 1.0, 0.0)
    sib_pts[0:TROWS, 0:SK] = (skel_t[0:TROWS, :] + hot).astype(BF16)

    ins[6].wait()
    flags = nfl[...].astype(F32)

    def flag_of(column):
        chosen = jnp.where(lane_ids(flags.shape) == column, flags, 0.0)
        return jnp.sum(chosen, axis=1, keepdims=True)

    def turned(block):
        return block.astype(F32).T.astype(BF16)

    rows = row_ids((16, SK))
    tail = jnp.where((rows >= 3) & (rows < 6), 1.0, 0.0)
    for j in range(3):
        tail = jnp.where(rows == j, skel_t[TAIL + 3 + j:TAIL + 4 + j, :], tail)
    listed = [flag_of(column) for column in range(5)]
    for j in range(5):
        tail = jnp.where(rows == 6 + j, listed[j], tail)
    tgt_in[0, 0:FEAT, :] = skel_t[0:FEAT, :].astype(BF16)
    tgt_in[0, FEAT:TROWS, :] = tail.astype(BF16)

    pl.semaphore_wait(barrier, len(friends) + z)

    def go(copy):
        copy.start()
        return copy

    def sib_block(i):
        return sib_pts.at[0:TROWS, i * SK:(i + 1) * SK]

    def sib_rows(i):
        return sib_mass.at[i * SK:(i + 1) * SK]

    def pass_sibling(i):
        return [
            go(remote(sib_block(i), sib_block(NX + i), bp_s.at[0], bp_r.at[0], partner)),
            go(remote(sib_rows(i), sib_rows(NX + i), bp_s.at[1], bp_r.at[1], partner)),
        ]

    def near_copies(slot_from, slot_to, n, device):
        return [
            remote(
                near_pts.at[slot_from, 0:TROWS], near_pts.at[slot_to, 0:TROWS],
                f_s.at[0], f_r.at[0, n], device,
            ),
        ] + [
            remote(
                near_mass.at[slot_from, h * LEAF // 2:(h + 1) * LEAF // 2],
                near_mass.at[slot_to, h * LEAF // 2:(h + 1) * LEAF // 2],
                f_s.at[1], f_r.at[1, n], device,
            )
            for h in range(2)
        ]

    f_partner = near_copies(0, 1, 0, partner)
    f_up = near_copies(0, 3, 1, beside(2))
    f_down = near_copies(0, 2, 2, beside(-2))
    f_last = near_copies(2 + c, 4, 3, partner)
    near_slot = (1, 3, 2, 4)

    def near_landed(n):
        all_landed(near_pts.at[near_slot[n], 0:TROWS], f_r.at[0, n])
        all_landed(near_mass.at[near_slot[n]], f_r.at[1, n])

    def start_if(wanted, copies):
        @pl.when(wanted)
        def _():
            for copy in copies:
                copy.start()

    def pass_target(slot, by):
        after = (slot + by) % NY
        return go(remote(
            tgt_in.at[slot], tgt_in.at[after], a_s, a_r.at[after], at_y(by)
        ))

    ax = {1: pass_target(0, 1), 7: pass_target(0, -1)}
    c1 = go(remote(c1_out, c1_in, c1_s, c1_r, partner))
    bx = [
        [
            go(remote(sib_block(0), sib_block(i), bx_s.at[0], bx_r.at[0, i], at_x(i))),
            go(remote(sib_rows(0), sib_rows(i), bx_s.at[1], bx_r.at[1, i], at_x(i))),
        ]
        for i in range(1, NX)
    ]
    pass_sibling(0)
    for copy in f_partner:
        copy.start()

    c1.wait_recv()
    for yy in range(NY):
        c2_out[yy] = (c_all[yy * NC + c] + c1_in[yy].astype(F32)).astype(BF16)
    order = (4, 3, 5, 2, 6, 1, 7)
    for k in order:
        go(remote(c2_out.at[lax.rem(y + k, NY)], c2_in.at[k], c2_s, c2_r, at_y(k)))
    def answer(other, carry):
        pl.semaphore_signal(ready, inc=1, device_id=(other, leaf), device_id_type=MESH)
        return carry

    lax.fori_loop(0, z, answer, 0)
    rows = row_ids((16, LEAF))
    tail = near_pts[0, FEAT:TROWS, :].astype(F32)
    ones = jnp.where((rows >= 3) & (rows < 6), 1.0, 0.0)
    tail = jnp.where(
        rows == 0, tail[3:4], jnp.where(rows == 1, tail[4:5], jnp.where(rows == 2, tail[5:6], ones))
    )
    near_tgt[...] = turned(jnp.concatenate(
        [near_pts[0, 0:FEAT, :].astype(F32), tail, jnp.zeros((LANES - TROWS, LEAF), F32)], axis=0
    ))

    def near_tile(slot_at, flag):
        gate = jnp.where(lane_ids((1, LANES)) == GATE, BIG * (1.0 - flag), 0.0).astype(BF16)
        exponent = jnp.dot(near_tgt[...] + gate, near_pts[slot_at], preferred_element_type=F32)
        return jnp.dot(
            jnp.exp(exponent).astype(BF16), near_mass[slot_at], preferred_element_type=F32
        )

    side = jnp.where(c == 0, 3, 1)
    near_columns = (2, side, 4, 0, 4 - side)

    def near_step(s):
        near_acc[...] += near_tile(s, flag_of(near_columns[s]))

    near_acc[...] = near_tile(0, listed[2])

    near_landed(0)
    near_step(1)
    ax[1].wait_recv()
    ax[2] = pass_target(1, 1)
    ax[7].wait_recv()
    ax[6] = pass_target(7, -1)
    wrap_up = remote(near_pts.at[0, 0:TROWS], wrap, w_s, w_r, at_y(1))
    wrap_down = remote(near_pts.at[0, 0:TROWS], wrap, w_s, w_r, at_y(-1))
    start_if(y == NY - 1, f_up[1:2])
    start_if(y == 0, f_down[1:2])
    def relay_sibling(i):
        for copy in bx[i - 1]:
            copy.wait_recv()
        pass_sibling(i)

    relay_sibling(3)
    relay_sibling(1)
    part = c_all[y * NC + c] + c1_in[y].astype(F32)
    all_landed(c2_in.at[1:], c2_r)
    for k in order:
        part = part + c2_in[k].astype(F32)
    d_out[...] = part.astype(BF16)
    ring = (1, 7, 2, 6, 3, 5, 4)
    groups = ((0, 4), (4, 7))

    def far_rows(half, g, i, first=0, last=None, count=1):
        blocks = groups[g][1] - groups[g][0]
        start = half * HALF + (groups[g][0] * NX + i * blocks) * PART
        last = blocks * count if last is None else last
        return far.at[start + first * PART:start + last * PART]

    @pl.when(z < NZ - 1)
    def _():
        pl.semaphore_wait(ready, NZ - 1 - z)

    for n, k in enumerate(ring):
        g = 0 if n < groups[0][1] else 1
        at = n - groups[g][0]
        go(remote(d_out, far_rows(0, g, 0, at, at + 1), dz_s, dz_r.at[g], at_z(k)))

    def pass_far(g, i, count):
        go(remote(
            far_rows(0, g, i, count=count), far_rows(1, g, i, count=count), dp_s, dp_r, partner
        ))

    def spread_far(g):
        all_landed(far_rows(0, g, 0), dz_r.at[g])
        for i in (2, 1, 3):
            go(remote(far_rows(0, g, 0), far_rows(0, g, i), dx_s, dx_r.at[g], at_x(i)))
        pass_far(g, 0, 1)

    def relay_far(g):
        all_landed(far_rows(0, g, 1, count=NX - 1), dx_r.at[g])
        pass_far(g, 1, NX - 1)

    ax[2].wait_recv()
    ax[3] = pass_target(2, 1)
    ax[6].wait_recv()
    ax[5] = pass_target(6, -1)
    relay_sibling(2)
    all_landed(sib_pts.at[0:TROWS, NX * SK:], bp_r.at[0])
    all_landed(sib_mass.at[NX * SK:], bp_r.at[1])
    slots = (4, 6, 2, 5, 3, 7, 1, 0)
    pad = jnp.zeros((LANES - TROWS, SK), F32)

    def sibling_step(p):
        at = slice(p * 2 * SK, (p + 1) * 2 * SK)
        for h in range(2):
            k = slots[p * 2 + h]
            tail = tgt_in[k, FEAT:TROWS, :].astype(F32)
            rows = row_ids((16, SK))
            slot = rows - 6
            other = lax.shift_right_logical(slot, 1) * (NY * NC) + y * NC + (slot & 1)
            column = other - place(x, lax.rem(y - k + NY, NY), c) + 2
            hidden = jnp.zeros((16, SK), F32)
            for j in range(5):
                hidden = jnp.where(column == j, tail[6 + j:7 + j, :], hidden)
            hidden = jnp.where(slot < NX * NC, BIG * hidden, 0.0)
            tail = jnp.where(slot < 0, tail, hidden)
            block = jnp.concatenate([tgt_in[k, 0:FEAT, :].astype(F32), tail, pad], axis=0)
            tgt[(p * 2 + h) * SK:(p * 2 + h + 1) * SK, :] = turned(block)
        exponent = jnp.dot(tgt[at, :], sib_pts[...], preferred_element_type=F32)
        acc[at, :] = jnp.dot(
            jnp.exp(exponent).astype(BF16), sib_mass[...], preferred_element_type=F32
        )

    sibling_step(3)
    spread_far(0)
    ax[3].wait_recv()
    ax[4] = pass_target(3, 1)
    start_if(y == NY - 1, [wrap_up])
    start_if(y == 0, [wrap_down])
    start_if(y < NY - 1, f_up)
    start_if(y > 0, f_down)
    sibling_step(2)
    spread_far(1)
    ax[5].wait_recv()
    sibling_step(1)
    relay_far(0)
    ax[4].wait_recv()
    sibling_step(0)
    @pl.when(y == 0)
    def _():
        wrap_up.wait_recv()
        remote(wrap, near_pts.at[3, 0:TROWS], f_s.at[0], f_r.at[0, 1], at_x(1)).start()

    @pl.when(y == NY - 1)
    def _():
        wrap_down.wait_recv()
        remote(wrap, near_pts.at[2, 0:TROWS], f_s.at[0], f_r.at[0, 2], at_x(NX - 1)).start()

    relay_far(1)

    start_if(y == NY - 1, f_up[2:])
    start_if(y == 0, f_down[2:])
    e_from = {3: 4, 1: 2, 7: 6}
    e_to = {4: -1, 2: -1, 6: 1, 5: 3, 3: -3, 7: 1, 1: -1}
    e_land = {4: 4, 2: 5, 6: 6, 5: 0, 3: 1, 7: 2, 1: 3}
    e_sem = {4: 1, 2: 2, 6: 3, 5: 0, 3: 0, 7: 0, 1: 0}
    ex = {
        k: remote(e_out.at[k], e_in.at[e_land[k]], e_s, e_r.at[e_sem[k]], at_y(by))
        for k, by in e_to.items()
    }

    def distant_step(p, first=0, last=DIST):
        at = slice(p * 2 * SK, (p + 1) * 2 * SK)
        acc[at, :] = acc[at, :] + tile_product(
            tgt[at, :], far[first:last, 0:LANES], far[first:last, LANES:]
        )

    def hand_on(k):
        row = slots.index(k) * SK
        block = acc[row:row + SK, :]
        if k in e_from:
            ex[e_from[k]].wait_recv()
            block = block + e_in[e_land[e_from[k]]].astype(F32)
        e_out[k] = block.astype(BF16)
        ex[k].start()

    distant_step(0, 0, HALF)
    all_landed(far.at[HALF:], dp_r)
    distant_step(0, HALF, DIST)
    hand_on(4)
    hand_on(6)
    distant_step(1)
    hand_on(5)
    hand_on(2)
    distant_step(2)
    hand_on(3)
    hand_on(7)
    distant_step(3)
    hand_on(1)
    near_landed(1)
    near_landed(2)
    for copy in f_last:
        copy.start()
    near_step(2)
    near_step(3)
    near_landed(3)
    near_step(4)

    row = slots.index(0) * SK
    phi = acc[row:row + SK, :]
    all_landed(e_in.at[0:4], e_r.at[0])
    for n in range(4):
        phi = phi + e_in[n].astype(F32)
    out_ref[...] = (
        near_acc[...] + jnp.dot(itp[...], phi.astype(BF16), preferred_element_type=F32)
    ).astype(BF16)

    c1.wait_send()
    all_landed(c2_out.at[1:], c2_s)
    all_landed(tgt_in.at[1:], a_s)
    all_landed(sib_pts.at[0:TROWS, SK:NX * SK], bx_s.at[0])
    all_landed(sib_mass.at[SK:NX * SK], bx_s.at[1])
    all_landed(sib_pts.at[0:TROWS, 0:NX * SK], bp_s.at[0])
    all_landed(sib_mass.at[0:NX * SK], bp_s.at[1])
    all_landed(far.at[0:(NZ - 1) * PART], dz_s)
    all_landed(far.at[0:(NX - 1) * (NZ - 1) * PART], dx_s)
    all_landed(far.at[0:HALF], dp_s)
    all_landed(near_pts.at[1:, 0:TROWS], f_s.at[0])
    all_landed(near_mass.at[1:], f_s.at[1])
    all_landed(e_out.at[1:], e_s)

    @pl.when((y == 0) | (y == NY - 1))
    def _():
        wrap_up.wait_send()


def on_device(points, weights, interp, cluster_interp, skeleton_rows, near_flags, cluster_rows):
    vmem, dma = pltpu.VMEM, pltpu.SemaphoreType.DMA
    return pl.pallas_call(
        kernel,
        out_shape=pltpu.VMEM(weights.shape, BF16),
        in_specs=[pl.BlockSpec(memory_space=pl.ANY)] * 7,
        out_specs=pl.BlockSpec(memory_space=pltpu.VMEM),
        scratch_shapes=[
            vmem((FEAT, LEAF), BF16),
            vmem((LEAF, SK), BF16),
            vmem((SK, CSK), BF16),
            vmem((1, SK), jnp.int32),
            vmem((1, 5), jnp.int32),
            vmem((NX, CSK), jnp.int32),
            vmem((5, LANES, LEAF), BF16),
            vmem((5, LEAF, LANES), BF16),
            vmem((LEAF, LANES), BF16),
            vmem((LEAF, LANES), F32),
            vmem((LANES, SK), F32),
            vmem((NY, TROWS, SK), BF16),
            vmem((NY * SK, LANES), BF16),
            vmem((LANES, SIB), BF16),
            vmem((SIB, LANES), BF16),
            vmem((DIST, 2 * LANES), BF16),
            vmem((NY * SK, LANES), F32),
            vmem((NY * NC, PART, 2 * LANES), F32),
            vmem((NY, PART, 2 * LANES), BF16),
            vmem((NY, PART, 2 * LANES), BF16),
            vmem((NY, PART, 2 * LANES), BF16),
            vmem((NY, PART, 2 * LANES), BF16),
            vmem((PART, 2 * LANES), BF16),
            vmem((NY, SK, LANES), BF16),
            vmem((NY, SK, LANES), BF16),
            vmem((TROWS, LEAF), BF16),
            dma((7,)),
            dma, dma,
            dma, dma,
            dma, dma((NY,)),
            dma((2,)), dma((2, NX)),
            dma((2,)), dma((2,)),
            dma, dma((2,)),
            dma, dma((2,)),
            dma, dma,
            dma((2,)), dma((2, 4)),
            dma, dma((4,)),
            dma, dma,
            pltpu.SemaphoreType.REGULAR,
        ],
        compiler_params=pltpu.CompilerParams(
            collective_id=0, has_side_effects=True, vmem_limit_bytes=60 << 20
        ),
        name="hier",
    )(points.T, weights, interp, cluster_interp, skeleton_rows, near_flags, cluster_rows)


def solution(mesh):
    placed = P(("group", "leaf"), None)
    return jax.shard_map(
        on_device,
        mesh=mesh,
        in_specs=(placed,) * 6 + (P("group", None),),
        out_specs=placed,
        check_vma=False,
    )
```
